256 devices in a mesh: seq: 64 (over x, z, core), head: 4 (over y).
Axes of the slice: x: 4, y: 4, z: 8, core: 2. Of those that a mesh axis runs over, the one named last changes fastest.
Arguments:
- frames: bfloat16 [16384, 1024], P('seq'), may hold values from -6 to 6
- norm_gain: float32 [1024], replicated, may hold values from 0.5 to 1.5
- w_qkv: bfloat16 [3, 1024, 1024], P(None, None, 'head'), may hold values from -2 to 2
- w_out: bfloat16 [1024, 1024], P('head'), may hold values from -0.1875 to 0.1875
- w_proj: bfloat16 [1024, 512], replicated, may hold values from -0.1875 to 0.1875
- text_table: bfloat16 [32768, 512], P(('seq', 'head')), may hold values from -6 to 6
- token_ids: int32 [512, 16], replicated, may hold values from 0 to 32767
- span_bounds: int32 [512, 2], P(('seq', 'head')), may hold values from 0 to 16384, as said below
- contrast_divisor: float32 [1], replicated, may hold values from 10 to 30
Outputs:
- interval_embedding_derivative: float32 [512, 512], P(('seq', 'head'))
- loss_terms: float32 [512], P(('seq', 'head'))
The draws below stay inside these ranges and needn't reach their ends.
Inputs may be any that keep to these rules, and one draw needn't show every extreme that they name: `span_bounds`: both entries are multiples of 128 and the first is smaller than the second.
All inputs are finite; a program needn't handle non-finite values.
Results may differ from the reference program's by a relative error of at most 0.006.
Values may be sent and summed in bfloat16 or wider, within the bound.
A program may use at most 64 MiB of HBM per device.

```python
import math
import jax
import jax.numpy as jnp
import numpy as np
from jax import lax

D = 1024
HEADS = 16
HDIM = 64
E = 512
VOCAB = 32768
CL = 16
BLK = 128
FR_DEV = 256
FRAMES = 16384
NBLK = 128
NCAP = 512


def draw_span_bounds(key, part):
    first_key, second_key, third_key = jax.random.split(jax.random.fold_in(key, 7), 3)
    starts = jax.random.randint(first_key, (NCAP,), 0, NBLK, dtype=jnp.int32)
    largest = (8 * (FR_DEV // BLK)).bit_length() - 1
    expo = jax.random.randint(second_key, (NCAP,), 0, largest + 1, dtype=jnp.int32)
    longest = jnp.left_shift(jnp.ones_like(expo), expo)
    lengths = 1 + jax.random.randint(third_key, (NCAP,), 0, longest, dtype=jnp.int32)
    starts = starts.at[0].set(0)
    ends = jnp.minimum(starts + lengths, NBLK)
    ends = ends.at[NCAP - 1].set(NBLK)
    return (jnp.stack([starts, ends], axis=1) * BLK).astype(jnp.int32)


def draw_w_qkv(key, part):
    base_key = jax.random.fold_in(jax.random.fold_in(key, 11), 0)
    entries = jnp.clip(jax.random.normal(base_key, (3, D, D), jnp.float32), -6.0, 6.0) * D ** (-0.5)
    return entries.astype(jnp.bfloat16)


def place_ends(drawn, rng, least, top_value):
    longest = drawn.shape.index(max(drawn.shape))
    spots = []
    for shift in (0, 1):
        where = [jax.random.randint(jax.random.fold_in(rng, axis), (), 0, length) for axis, length in enumerate(drawn.shape)]
        where[longest] = (where[longest] + shift) % drawn.shape[longest]
        spots.append(tuple(where))
    return drawn.at[spots[0]].set(least).at[spots[1]].set(top_value)


def steps_of(rng, extent, shards, smallest, high):
    level, own = 1.0, jax.random.fold_in(rng, 6)
    for axis_at, blocks in shards:
        steps = jnp.exp(jax.random.uniform(jax.random.fold_in(own, axis_at), (blocks,), jnp.float32, smallest / len(shards), high / len(shards)))
        level = level * jnp.repeat(steps, extent[axis_at] // blocks).reshape([-1 if axis == axis_at else 1 for axis in range(len(extent))])
    return level


def cumulative_ranks(amount, lean):
    loads = [(1 << 20) // math.isqrt(grade ** lean) + 1 for grade in range(1, amount + 1)]
    width = 1 + sum(loads) // (1 << 30)
    return np.cumsum(np.array([max(1, weight // width) for weight in loads]))


def ranked(key, shape, number_of, slope):
    listing = cumulative_ranks(number_of, slope)
    pick = jax.random.randint(jax.random.fold_in(key, 1), shape, 0, int(listing[number_of - 1]))
    grade = jnp.searchsorted(jnp.asarray(listing, jnp.int32), pick, side="right")
    return jax.random.permutation(jax.random.fold_in(key, 2), number_of)[grade].astype(jnp.int32)


def normal_values(own_key, shape, scale, bound, shards=(), held_as=jnp.bfloat16):
    level = steps_of(own_key, shape, shards, -0.22, 0.18) if shards else 1.0
    array = jax.random.normal(own_key, shape, jnp.float32) * scale * level
    return jnp.minimum(jnp.maximum(array, -bound), bound).astype(held_as)


def setup_inputs(seed: int = 0) -> dict:
    streams_of = jax.random.split(jax.random.key(seed), 10)
    return {
        "frames": normal_values(streams_of[0], (FRAMES, D), 1.0, 6.0, ((0, 64),)),
        "norm_gain": jnp.clip(1.0 + 0.1 * jax.random.normal(streams_of[1], (D,), jnp.float32), 0.5, 1.5),
        "w_qkv": draw_w_qkv(jax.random.fold_in(streams_of[9], 71), 0),
        "w_out": normal_values(streams_of[3], (D, D), D ** -0.5, 0.1875, ((0, 4),)),
        "w_proj": normal_values(streams_of[4], (D, E), D ** -0.5, 0.1875),
        "text_table": normal_values(streams_of[5], (VOCAB, E), 1.0, 6.0, ((0, 256),)),
        "token_ids": place_ends(ranked(streams_of[6], (NCAP, CL), VOCAB, 2), jax.random.fold_in(streams_of[6], 3), 0, VOCAB - 1).astype(jnp.int32),
        "span_bounds": draw_span_bounds(jax.random.fold_in(streams_of[9], 71), 0),
        "contrast_divisor": jnp.clip(jnp.exp(jax.random.uniform(streams_of[8], (1,), jnp.float32, math.log(10.0), math.log(30.0))), 10.0, 30.0),
    }


def log_total(values, axis):
    return jnp.log(lax.optimization_barrier(jnp.sum(jnp.exp(values), axis=axis)))

def unit_rows(values):
    return values * lax.rsqrt(lax.optimization_barrier(jnp.mean(values * values, axis=-1, keepdims=True)) + 1e-06) * E ** (-0.5)

def reference(frames, norm_gain, w_qkv, w_out, w_proj, text_table, token_ids, span_bounds, contrast_divisor):
    as32 = frames.astype(jnp.float32)
    normed = (as32 * lax.rsqrt(lax.optimization_barrier(jnp.mean(as32 * as32, axis=-1, keepdims=True)) + 1e-05) * norm_gain).astype(jnp.bfloat16)
    queries = jnp.dot(normed, w_qkv[0], preferred_element_type=jnp.float32).astype(jnp.bfloat16)
    keys_all = jnp.dot(normed, w_qkv[1], preferred_element_type=jnp.float32).astype(jnp.bfloat16)
    values_all = jnp.dot(normed, w_qkv[2], preferred_element_type=jnp.float32).astype(jnp.bfloat16)
    query_block = min(512, FR_DEV)
    span_width = 2 * FR_DEV + query_block
    keys_pad = jnp.pad(keys_all, ((FR_DEV, FR_DEV), (0, 0)))
    values_pad = jnp.pad(values_all, ((FR_DEV, FR_DEV), (0, 0)))

    def attend(block):
        begin = (block * query_block).astype(jnp.int32)
        query_part = lax.dynamic_slice_in_dim(queries, begin, query_block, 0).astype(jnp.float32).reshape(query_block, HEADS, HDIM)
        key_part = lax.dynamic_slice_in_dim(keys_pad, begin, span_width, 0).astype(jnp.float32).reshape(span_width, HEADS, HDIM)
        value_part = lax.dynamic_slice_in_dim(values_pad, begin, span_width, 0).astype(jnp.float32).reshape(span_width, HEADS, HDIM)
        scores = jnp.einsum('qhd,khd->hqk', query_part, key_part) * HDIM ** (-0.5)
        query_pos = begin + jnp.arange(query_block, dtype=jnp.int32)
        key_pos = begin - FR_DEV + jnp.arange(span_width, dtype=jnp.int32)
        allowed = (jnp.abs(query_pos[:, None] - key_pos[None, :]) <= FR_DEV) & (key_pos >= 0)[None, :] & (key_pos < FRAMES)[None, :]
        scores = jnp.where(allowed[None], scores, -1e+30)
        top = lax.optimization_barrier(jnp.max(scores, axis=2, keepdims=True))
        probs = jnp.exp(scores - top)
        denom = lax.optimization_barrier(jnp.sum(probs, axis=2))
        weights = probs.astype(jnp.bfloat16).astype(jnp.float32)
        mixed = jnp.einsum('hqk,khd->qhd', weights, value_part)
        return (mixed / denom.T[:, :, None]).astype(jnp.bfloat16).reshape(query_block, D)
    attended = lax.map(attend, jnp.arange(FRAMES // query_block, dtype=jnp.int32)).reshape(FRAMES, D)
    residual = as32 + jnp.dot(attended, w_out, preferred_element_type=jnp.float32)
    block_sums = residual.reshape(NBLK, BLK, D).sum(axis=1)
    block_table = jnp.dot(block_sums, w_proj.astype(jnp.float32), precision=lax.Precision.HIGHEST)
    block_ids = jnp.arange(NBLK, dtype=jnp.int32)
    lower = span_bounds[:, 0] // BLK
    upper = span_bounds[:, 1] // BLK
    span_mask = ((block_ids[None, :] >= lower[:, None]) & (block_ids[None, :] < upper[:, None])).astype(jnp.float32)
    pooled = jnp.dot(span_mask, block_table, precision=lax.Precision.HIGHEST)
    interval_embedding_rows = unit_rows(pooled).astype(jnp.bfloat16)
    raw = lax.optimization_barrier(jnp.sum(jnp.take(text_table, token_ids, axis=0).astype(jnp.float32), axis=1))
    text_embedding_rows = unit_rows(raw).astype(jnp.bfloat16)
    normalizer_divisor = contrast_divisor[0]
    pairwise_affinity_logits = jnp.dot(text_embedding_rows, interval_embedding_rows.T, preferred_element_type=jnp.float32) * normalizer_divisor
    row_lse = log_total(pairwise_affinity_logits, 1)
    col_lse = log_total(pairwise_affinity_logits, 0)
    loss_terms = 0.5 * (row_lse + col_lse) - jnp.diagonal(pairwise_affinity_logits)
    marker = jnp.eye(NCAP, dtype=jnp.float32)
    derivative_multipliers = (0.5 * jnp.exp(pairwise_affinity_logits - row_lse[:, None]) + 0.5 * jnp.exp(pairwise_affinity_logits - col_lse[None, :]) - marker).astype(jnp.bfloat16)
    interval_embedding_derivative = jnp.dot(derivative_multipliers.T, text_embedding_rows, preferred_element_type=jnp.float32) * normalizer_divisor
    return (interval_embedding_derivative, loss_terms)
```

```python
import functools

import jax
import jax.numpy as jnp
from jax import lax
from jax.experimental import pallas as pl
from jax.experimental.pallas import tpu as pltpu
from jax.sharding import PartitionSpec as P

HDIM = 64
E = 512
BLK = 128
F = 256
D = 1024
HC = 256
LH = HC // HDIM
CAPS = 512
ZL = 16
NX, NY, NZ = 4, 4, 8
XY = NX * NY
MESH = pl.DeviceIdType.MESH
F32, BF16 = jnp.float32, jnp.bfloat16
NT = (((1,), (1,)), ((), ()))
NN = (((1,), (0,)), ((), ()))


def dot(a, b, dims=NN):
    return lax.dot_general(a, b, dims, preferred_element_type=F32)


def dot_split(a, b):
    hi = a.astype(BF16)
    lo = (a - hi.astype(F32)).astype(BF16)
    both = dot(jnp.concatenate([hi, lo], axis=0), b)
    n = a.shape[0]
    return both[:n] + both[n:]


def kernel(
    frames_h, gain_h, wqkv_h, wout_h, wproj_h, table_h, ids_h, bounds_s, div_s,
    grad_ref, loss_ref,
    frames, gain, wk, wv, wq, wout, wproj, tab, ids,
    k_own, vt_own, k_halo, vt_halo, acc_scr, ml_scr, att,
    rs_src, rs_buf, zb_src, zb_buf, caps,
    t1_src, t1_buf, t2_f, t2_src, t2_buf,
    spans, lt,
    ld, kv_s, kv_r, tab_sem, rs_s, rs_r, zb_s, zb_r, ag_s, ag_r, rl_s, rl_r,
    t1_s, t1_r, t2_s, t2_r,
):
    seq, head = lax.axis_index("seq"), lax.axis_index("head")
    core = lax.rem(seq, 2)
    zl = lax.rem(seq, ZL)
    xpos = lax.div(seq, ZL)
    zpos = lax.div(zl, 2)
    xy = xpos * NY + head
    slot = seq * NY + head
    partner = (seq + 1 - 2 * core, head)

    def z_dev(t):
        return (xpos * ZL + t, head)

    def xy_dev(t):
        return (lax.div(t, NY) * ZL + zl, lax.rem(t, NY))

    loads = [
        pltpu.make_async_copy(ids_h.at[:, pl.ds(core * 256, 256)], ids, ld.at[0]),
        pltpu.make_async_copy(frames_h, frames, ld.at[1]),
        pltpu.make_async_copy(gain_h, gain, ld.at[2]),
        pltpu.make_async_copy(wqkv_h.at[1], wk, ld.at[3]),
        pltpu.make_async_copy(wqkv_h.at[2], wv, ld.at[4]),
        pltpu.make_async_copy(wqkv_h.at[0], wq, ld.at[5]),
        pltpu.make_async_copy(table_h, tab.at[core], ld.at[6]),
        pltpu.make_async_copy(wout_h, wout, ld.at[7]),
        pltpu.make_async_copy(wproj_h, wproj, ld.at[8]),
    ]
    for c in loads:
        c.start()

    barrier = pltpu.get_barrier_semaphore()

    def greet(k, _):
        pl.semaphore_signal(
            barrier, inc=1, device_id=z_dev(lax.rem(zl + k, ZL)), device_id_type=MESH
        )
        pl.semaphore_signal(
            barrier, inc=1, device_id=xy_dev(lax.rem(xy + k, XY)), device_id_type=MESH
        )
        return 0

    lax.fori_loop(1, XY, greet, 0)
    line_end = jnp.logical_and(zl == ZL - 1, xpos < NX - 1)
    line_start = jnp.logical_and(zl == 0, xpos > 0)

    @pl.when(line_end)
    def _():
        pl.semaphore_signal(barrier, inc=1, device_id=(seq + 1, head), device_id_type=MESH)

    @pl.when(line_start)
    def _():
        pl.semaphore_signal(barrier, inc=1, device_id=(seq - 1, head), device_id_type=MESH)

    loads[0].wait()
    lane = lax.broadcasted_iota(jnp.int32, (256, 256), 1)
    first_slot = slot - core * NY
    vocab = (first_slot + NY * lax.div(lane, 128)) * 128 + lax.rem(lane, 128)
    tokens = ids[...].T
    counts = jnp.zeros((256, 256), F32)
    for t in range(16):
        counts = counts + jnp.where(tokens[:, t : t + 1] == vocab, 1.0, 0.0)
    counts = counts.astype(BF16)

    loads[1].wait()
    loads[2].wait()
    x32 = frames[...].astype(F32)
    scale = lax.rsqrt(jnp.sum(x32 * x32, axis=1, keepdims=True) * (1.0 / D) + 1e-5)
    normed = (x32 * scale * gain[...]).astype(BF16)
    loads[3].wait()
    k_own[...] = dot(normed, wk[...]).astype(BF16)
    loads[4].wait()
    vt_own[...] = dot(normed, wv[...]).T.astype(BF16)

    extra = line_end.astype(jnp.int32) + line_start.astype(jnp.int32)
    pl.semaphore_wait(barrier, 2 * (XY - 1) + extra)

    def halo(side, part):
        target = (seq + 1 - 2 * side, head)
        src, dst = ((k_own, k_halo), (vt_own, vt_halo))[part]
        return pltpu.make_async_remote_copy(
            src_ref=src, dst_ref=dst.at[side],
            send_sem=kv_s.at[2 * side + part], recv_sem=kv_r.at[2 * side + part],
            device_id=target, device_id_type=MESH,
        )

    last = NX * ZL - 1
    for part in (0, 1):
        @pl.when(seq < last)
        def _():
            halo(0, part).start()

        @pl.when(seq > 0)
        def _():
            halo(1, part).start()

    tab_copy = pltpu.make_async_remote_copy(
        src_ref=table_h, dst_ref=tab.at[core],
        send_sem=tab_sem.at[0], recv_sem=tab_sem.at[1],
        device_id=partner, device_id_type=MESH,
    )
    tab_copy.start()

    @pl.when(seq == 0)
    def _():
        k_halo[0] = jnp.zeros((F, HC), BF16)
        vt_halo[0] = jnp.zeros((HC, F), BF16)

    @pl.when(seq == last)
    def _():
        k_halo[1] = jnp.zeros((F, HC), BF16)
        vt_halo[1] = jnp.zeros((HC, F), BF16)

    loads[5].wait()
    q = (dot(normed, wq[...]).astype(BF16).astype(F32) * HDIM ** (-0.5)).astype(BF16)
    qm = [
        jnp.where(lax.div(lane, HDIM) == h, q.astype(F32), 0.0).astype(BF16) for h in range(LH)
    ]
    for h in range(LH):
        s = dot(k_own[...], qm[h], NT)
        m = jnp.max(s, axis=0, keepdims=True)
        p = jnp.exp(s - m)
        ml_scr[h, 0:1] = m
        ml_scr[h, 1:2] = jnp.sum(p, axis=0, keepdims=True)
        acc_scr[pl.ds(h * HDIM, HDIM), :] = dot(vt_own[pl.ds(h * HDIM, HDIM), :], p.astype(BF16))

    loads[6].wait()
    tab_copy.wait_recv()
    part_sums = dot(counts, tab[...].reshape(256, E))
    rs_src[...] = part_sums.astype(BF16).reshape(XY, 16, E)

    def rs_copy(target, here):
        return pltpu.make_async_remote_copy(
            src_ref=rs_src.at[target], dst_ref=rs_buf.at[here],
            send_sem=rs_s.at[target], recv_sem=rs_r.at[here],
            device_id=xy_dev(target), device_id_type=MESH,
        )

    def rs_start(k, _):
        rs_copy(lax.rem(xy + k, XY), xy).start()
        return 0

    lax.fori_loop(1, XY, rs_start, 0)
    rs_buf[pl.ds(xy, 1)] = rs_src[pl.ds(xy, 1)]

    @pl.when(seq > 0)
    def _():
        halo(0, 0).wait_recv()

    @pl.when(seq < last)
    def _():
        halo(1, 0).wait_recv()

    key_id = lax.broadcasted_iota(jnp.int32, (F, F), 0)
    left_ok = jnp.logical_and(key_id >= lane, seq > 0)
    right_ok = jnp.logical_and(key_id <= lane, seq < last)

    @pl.when(seq > 0)
    def _():
        halo(0, 1).wait_recv()

    @pl.when(seq < last)
    def _():
        halo(1, 1).wait_recv()

    for h in range(LH):
        rows = pl.ds(h * HDIM, HDIM)
        sl = jnp.where(left_ok, dot(k_halo[0], qm[h], NT), -1e30)
        sr = jnp.where(right_ok, dot(k_halo[1], qm[h], NT), -1e30)
        m0, l0 = ml_scr[h, 0:1], ml_scr[h, 1:2]
        m = jnp.maximum(m0, jnp.max(jnp.maximum(sl, sr), axis=0, keepdims=True))
        pleft, pright = jnp.exp(sl - m), jnp.exp(sr - m)
        alpha = jnp.exp(m0 - m)
        total = l0 * alpha + jnp.sum(pleft + pright, axis=0, keepdims=True)
        acc = (
            acc_scr[rows, :] * alpha
            + dot(vt_halo[0, rows, :], pleft.astype(BF16))
            + dot(vt_halo[1, rows, :], pright.astype(BF16))
        )
        att[rows, :] = (acc * (1.0 / total)).astype(BF16)

    row8 = lax.broadcasted_iota(jnp.int32, (8, F), 0)
    pick = jnp.where(lax.div(lax.broadcasted_iota(jnp.int32, (8, F), 1), BLK) == row8, 1.0, 0.0)
    pick = pick.astype(BF16)
    loads[7].wait()
    loads[8].wait()
    out_sums = dot(pick, att[...], NT)
    frame_sums = dot(pick, frames[...])
    own_cols = lax.div(lax.broadcasted_iota(jnp.int32, (8, D), 1), HC) == head
    through = dot_split(out_sums, wout[...]) + jnp.where(own_cols, frame_sums, 0.0)
    partial = dot_split(through, wproj[...])
    lane_e = lax.broadcasted_iota(jnp.int32, (8, E), 1)
    row_e = lax.broadcasted_iota(jnp.int32, (8, E), 0)
    for r in range(2):
        for side in range(2):
            edge = lax.div(bounds_s[r, side], BLK).astype(F32)
            partial = jnp.where(
                jnp.logical_and(row_e == 2 + side, lane_e == slot * 2 + r), edge, partial
            )
    t1_src[...] = partial[:4]

    def t1_copy(target, here):
        return pltpu.make_async_remote_copy(
            src_ref=t1_src, dst_ref=t1_buf.at[here],
            send_sem=t1_s.at[target], recv_sem=t1_r.at[here],
            device_id=xy_dev(target), device_id_type=MESH,
        )

    def t1_start(k, _):
        t1_copy(lax.rem(xy + k, XY), xy).start()
        return 0

    lax.fori_loop(1, XY, t1_start, 0)
    t1_buf[pl.ds(xy, 1)] = partial[:4].reshape(1, 4, E)

    def rs_wait(k, _):
        rs_copy(xy, lax.rem(xy + k, XY)).wait_recv()
        return 0

    lax.fori_loop(1, XY, rs_wait, 0)
    zb_src[...] = jnp.sum(rs_buf[...].astype(F32), axis=0).astype(BF16)

    def zb_copy(target, here):
        return pltpu.make_async_remote_copy(
            src_ref=zb_src, dst_ref=zb_buf.at[here],
            send_sem=zb_s.at[target], recv_sem=zb_r.at[here],
            device_id=z_dev(target * 2 + core), device_id_type=MESH,
        )

    def zb_start(k, _):
        zb_copy(lax.rem(zpos + k, NZ), zpos).start()
        return 0

    lax.fori_loop(1, NZ, zb_start, 0)
    zb_buf[pl.ds(zpos, 1)] = zb_src[...].reshape(1, 16, E)

    def t1_wait(k, _):
        t1_copy(xy, lax.rem(xy + k, XY)).wait_recv()
        return 0

    lax.fori_loop(1, XY, t1_wait, 0)
    t2_f[...] = jnp.zeros((16, E), F32)
    edges = jnp.zeros((4, E), F32)
    for xx in range(NX):
        tot = jnp.sum(t1_buf[pl.ds(xx * NY, NY)], axis=0)
        t2_f[pl.ds(2 * xx, 2), :] = tot[0:2]
        edges = edges + tot
    t2_f[pl.ds(8, 2), :] = edges[2:4]
    t2_src[...] = t2_f[...].astype(BF16)

    def t2_copy(target, here):
        return pltpu.make_async_remote_copy(
            src_ref=t2_src, dst_ref=t2_buf.at[here],
            send_sem=t2_s.at[target], recv_sem=t2_r.at[here],
            device_id=z_dev(target), device_id_type=MESH,
        )

    def t2_start(k, _):
        t2_copy(lax.rem(zl + k, ZL), zl).start()
        return 0

    lax.fori_loop(1, ZL, t2_start, 0)
    t2_buf[pl.ds(zl, 1)] = t2_f[...].astype(BF16).reshape(1, 16, E)

    def zb_wait(k, _):
        zb_copy(zpos, lax.rem(zpos + k, NZ)).wait_recv()
        return 0

    lax.fori_loop(1, NZ, zb_wait, 0)

    def unit_rows(v):
        mean = jnp.sum(v * v, axis=1, keepdims=True) * (1.0 / E)
        return v * lax.rsqrt(mean + 1e-6) * E ** (-0.5)

    own = unit_rows(jnp.sum(zb_buf[...].astype(F32), axis=0)).astype(BF16)
    caps[pl.ds(core * XY + xy, 1)] = own.reshape(1, 16, E)

    def ag_copy(target, here):
        piece = caps.at[core * XY + here]
        return pltpu.make_async_remote_copy(
            src_ref=piece, dst_ref=piece, send_sem=ag_s.at[target], recv_sem=ag_r.at[here],
            device_id=xy_dev(target), device_id_type=MESH,
        )

    def rl_copy(here, side):
        piece = caps.at[side * XY + here]
        return pltpu.make_async_remote_copy(
            src_ref=piece, dst_ref=piece, send_sem=rl_s.at[here], recv_sem=rl_r.at[here],
            device_id=partner, device_id_type=MESH,
        )

    def ag_start(k, _):
        ag_copy(lax.rem(xy + k, XY), xy).start()
        return 0

    lax.fori_loop(1, XY, ag_start, 0)
    rl_copy(xy, core).start()

    def t2_wait(k, _):
        t2_copy(zl, lax.rem(zl + k, ZL)).wait_recv()
        return 0

    lax.fori_loop(1, ZL, t2_wait, 0)
    t2_all = t2_buf[...]
    edges = jnp.sum(t2_all.astype(F32), axis=0)[8:16]
    edges_t = edges.T
    col = lax.broadcasted_iota(jnp.int32, (BLK, 256), 1)
    sub = lax.rem(col, 16)
    block = lax.div(sub, 2) * (2 * ZL) + lax.div(col, 16) * 2 + lax.rem(sub, 2)
    block = jnp.where(sub < 8, block, -1).astype(F32)
    t2_flat = t2_all.reshape(256, E)
    for b in range(4):
        lower = edges_t[b * BLK : (b + 1) * BLK, 0:1]
        upper = edges_t[b * BLK : (b + 1) * BLK, 1:2]
        mask = jnp.where(
            jnp.logical_and(block >= lower, jnp.logical_and(block < upper, block >= 0.0)), 1.0, 0.0
        ).astype(BF16)
        spans[pl.ds(b * BLK, BLK), :] = unit_rows(dot(mask, t2_flat)).astype(BF16)

    def ag_wait(k, _):
        s = lax.rem(xy + k, XY)
        ag_copy(xy, s).wait_recv()
        rl_copy(s, core).start()
        return 0

    lax.fori_loop(1, XY, ag_wait, 0)

    def rl_wait(k, _):
        rl_copy(k, 1 - core).wait_recv()
        return 0

    lax.fori_loop(0, XY, rl_wait, 0)

    divisor = div_s[0]
    all_caps = caps[...].reshape(CAPS, E)
    row_sum = jnp.zeros((1, CAPS), F32)
    for b in range(4):
        part = dot(spans[pl.ds(b * BLK, BLK), :], all_caps, NT) * divisor
        lt[pl.ds(b * BLK, BLK), :] = part
        row_sum = row_sum + jnp.sum(jnp.exp(part), axis=0, keepdims=True)
    mine = lt[pl.ds(pl.multiple_of(seq * 8, 8), 8), :]
    expd = jnp.exp(mine)
    col_sum = jnp.sum(expd, axis=1, keepdims=True)
    is_diag = lane_e == row_e + seq * 8
    weights = (
        0.5 * expd * (1.0 / row_sum)
        + 0.5 * expd * (1.0 / col_sum)
        - jnp.where(is_diag, 1.0, 0.0)
    ).astype(BF16)
    grads = dot(weights, all_caps) * divisor
    losses = jnp.where(is_diag, 0.5 * (jnp.log(row_sum) + jnp.log(col_sum)) - mine, 0.0)
    out_lane = lax.broadcasted_iota(jnp.int32, (1, 128), 1)
    loss_row = jnp.zeros((1, 128), F32)
    for r in range(2):
        chosen = row_e == 2 * head + r
        grad_ref[r : r + 1, :] = jnp.sum(jnp.where(chosen, grads, 0.0), axis=0, keepdims=True)
        here = jnp.where(chosen, losses, 0.0)
        value = jnp.sum(jnp.sum(here, axis=0, keepdims=True), axis=1, keepdims=True)
        loss_row = jnp.where(out_lane == r, value, loss_row)
    loss_ref[...] = loss_row

    for part in (0, 1):
        @pl.when(seq < last)
        def _():
            halo(0, part).wait_send()

        @pl.when(seq > 0)
        def _():
            halo(1, part).wait_send()

    tab_copy.wait_send()

    def drain_xy(k, _):
        t = lax.rem(xy + k, XY)
        rs_copy(t, xy).wait_send()
        t1_copy(t, xy).wait_send()
        ag_copy(t, xy).wait_send()
        t2_copy(lax.rem(zl + k, ZL), zl).wait_send()
        rl_copy(t, core).wait_send()
        return 0

    lax.fori_loop(1, XY, drain_xy, 0)
    rl_copy(xy, core).wait_send()

    def drain_z(k, _):
        zb_copy(lax.rem(zpos + k, NZ), zpos).wait_send()
        return 0

    lax.fori_loop(1, NZ, drain_z, 0)


def local(
    frames, norm_gain, w_qkv, w_out, w_proj, text_table, token_ids, span_bounds, contrast_divisor
):
    any_spec = pl.BlockSpec(memory_space=pltpu.HBM)
    smem = pl.BlockSpec(memory_space=pltpu.SMEM)
    vmem = pl.BlockSpec(memory_space=pltpu.VMEM)
    dma = pltpu.SemaphoreType.DMA
    grad, loss = pl.pallas_call(
        kernel,
        out_shape=(
            jax.ShapeDtypeStruct((2, E), F32),
            jax.ShapeDtypeStruct((1, 128), F32),
        ),
        in_specs=[any_spec] * 7 + [smem] * 2,
        out_specs=(vmem, vmem),
        scratch_shapes=[
            pltpu.VMEM((F, D), BF16),
            pltpu.VMEM((1, D), F32),
            pltpu.VMEM((D, HC), BF16),
            pltpu.VMEM((D, HC), BF16),
            pltpu.VMEM((D, HC), BF16),
            pltpu.VMEM((HC, D), BF16),
            pltpu.VMEM((D, E), BF16),
            pltpu.VMEM((2, 128, E), BF16),
            pltpu.VMEM((16, 256), jnp.int32),
            pltpu.VMEM((F, HC), BF16),
            pltpu.VMEM((HC, F), BF16),
            pltpu.VMEM((2, F, HC), BF16),
            pltpu.VMEM((2, HC, F), BF16),
            pltpu.VMEM((HC, F), F32),
            pltpu.VMEM((LH, 8, F), F32),
            pltpu.VMEM((HC, F), BF16),
            pltpu.VMEM((XY, 16, E), BF16),
            pltpu.VMEM((XY, 16, E), BF16),
            pltpu.VMEM((16, E), BF16),
            pltpu.VMEM((NZ, 16, E), BF16),
            pltpu.VMEM((2 * XY, 16, E), BF16),
            pltpu.VMEM((4, E), F32),
            pltpu.VMEM((XY, 4, E), F32),
            pltpu.VMEM((16, E), F32),
            pltpu.VMEM((16, E), BF16),
            pltpu.VMEM((ZL, 16, E), BF16),
            pltpu.VMEM((CAPS, E), BF16),
            pltpu.VMEM((CAPS, CAPS), F32),
            dma((9,)),
            dma((4,)), dma((4,)),
            dma((2,)),
            dma((XY,)), dma((XY,)),
            dma((NZ,)), dma((NZ,)),
            dma((XY,)), dma((XY,)),
            dma((XY,)), dma((XY,)),
            dma((XY,)), dma((XY,)),
            dma((ZL,)), dma((ZL,)),
        ],
        compiler_params=pltpu.CompilerParams(
            collective_id=0, has_side_effects=True, vmem_limit_bytes=67043328
        ),
        name="spans",
    )(
        frames, norm_gain.reshape(1, D), w_qkv, w_out, w_proj, text_table, token_ids.T,
        span_bounds, contrast_divisor,
    )
    return grad, loss[0, :2]


def solution(mesh):
    placed = (
        P("seq", None),
        P(),
        P(None, None, "head"),
        P("head", None),
        P(),
        P(("seq", "head"), None),
        P(),
        P(("seq", "head"), None),
        P(),
    )
    return jax.shard_map(
        local,
        mesh=mesh,
        in_specs=placed,
        out_specs=(P(("seq", "head"), None), P(("seq", "head"))),
        check_vma=False,
    )
```
